32 devices in a mesh: dp: 8 (over z, y), shard: 4 (over x, core).
Axes of the slice: x: 2, y: 2, z: 4, core: 2. Of those that a mesh axis runs over, the one named last changes fastest.
Arguments:
- tokens: bfloat16 [12288, 576], P(('dp', 'shard')), may hold values from -6 to 6
- positions: int32 [8, 1536], P('dp', 'shard'), may hold values from 0 to 1535, as said below
- attn_gain: bfloat16 [576], P('shard'), may hold values from 0.25 to 1.75
- w_query: bfloat16 [576, 576], P('shard'), as said below
- w_key: bfloat16 [576, 192], P('shard'), may hold values from -0.25 to 0.25
- w_value: bfloat16 [576, 192], P('shard'), may hold values from -0.25 to 0.25
- w_out: bfloat16 [576, 576], P(None, 'shard'), may hold values from -2 to 2
- mlp_gain: bfloat16 [576], P('shard'), may hold values from 0.25 to 1.75
- w_gate: bfloat16 [576, 1536], P(None, 'shard'), may hold values from -0.25 to 0.25
- w_up: bfloat16 [576, 1536], P(None, 'shard'), may hold values from -0.25 to 0.25
- w_down: bfloat16 [1536, 576], P('shard'), may hold values from -0.15625 to 0.15625
- cotangent: bfloat16 [12288, 576], P(('dp', 'shard')), may hold values from -6 to 6
Outputs:
- output: bfloat16 [12288, 576], P(('dp', 'shard'))
- grad_tokens: float32 [12288, 576], P(('dp', 'shard'))
- grad_attn_gain: float32 [576], P('shard')
- grad_query: float32 [576, 576], P('shard')
- grad_key: float32 [576, 192], P('shard')
- grad_value: float32 [576, 192], P('shard')
- grad_out: float32 [576, 576], P(None, 'shard')
- grad_mlp_gain: float32 [576], P('shard')
- grad_gate: float32 [576, 1536], P(None, 'shard')
- grad_up: float32 [576, 1536], P(None, 'shard')
- grad_down: float32 [1536, 576], P('shard')
The draws below stay inside these ranges and needn't reach their ends.
Inputs may be any that keep to these rules, and one draw needn't show every extreme that they name: `positions`: along each row a position is 0 where a document begins and otherwise one more than the position before it; every row begins a document at its first token; row 0 is a single document. `w_query`: entries within a bound; the columns of a head may share a scale factor.
All inputs are finite; a program needn't handle non-finite values.
Results may differ from the reference program's by a relative error of at most 0.015.
The reference program's roundings to bfloat16 on the way count: a program that leaves them out, or rounds other values in their place, can miss the bound.
Values may be sent and summed in bfloat16 or wider, within the bound.
No kernel may reach another device: no remote copies, remote signals or barrier semaphores. Data moves between devices by JAX's collectives and lax.ppermute only.
A program may use at most 128 MiB of HBM per device.

```python
import jax
import jax.numpy as jnp
from jax import lax

D = 576
H = 9
KVH = 3
HD = 64
FF = 1536
SEQ = 1536
SEQS = 8
TOKENS = 12288
QW = 576
KW = 192


def draw_positions(key, part):
    index = jnp.arange(SEQ, dtype=jnp.int32)[None, :]
    lines = jnp.arange(SEQS, dtype=jnp.int32)[:, None]
    picks = jax.random.randint(key, (SEQS, SEQ), 0, SEQ // 3 + 1)
    begins = (picks == 0) | (index == 0)
    begins = begins & ((lines > 0) | (index == 0))
    latest = lax.cummax(jnp.where(begins, index, 0), axis=1)
    return (index - latest).astype(jnp.int32)


def draw_w_query(key, part):
    base = jnp.clip(jax.random.normal(key, (D, QW), jnp.float32), -4.0, 4.0) * D ** (-0.5)
    return base.astype(jnp.bfloat16)


def block_levels(rng, extent, shards, least, top_value):
    level, own = 1.0, jax.random.fold_in(rng, 6)
    for dim, blocks in shards:
        steps = jnp.exp(jax.random.uniform(jax.random.fold_in(own, dim), (blocks,), jnp.float32, least / len(shards), top_value / len(shards)))
        level = level * jnp.repeat(steps, extent[dim] // blocks).reshape([-1 if axis == dim else 1 for axis in range(len(extent))])
    return level


def noise(stream_key, extent, scale, reach, cuts=(), kind=jnp.bfloat16):
    factor_of = block_levels(stream_key, extent, cuts, -0.22, 0.18) if cuts else 1.0
    array = jax.random.normal(stream_key, extent, jnp.float32) * scale * factor_of
    return jnp.minimum(jnp.maximum(array, -reach), reach).astype(kind)


def setup_inputs(seed: int = 0) -> dict:
    key_of = jax.random.split(jax.random.key(seed), 13)
    return {
        "tokens": noise(key_of[0], (TOKENS, D), 1.0, 6.0, ((0, 32),)),
        "positions": draw_positions(jax.random.fold_in(key_of[12], 71), 0),
        "attn_gain": jnp.clip(1.0 + 0.15 * jax.random.normal(key_of[2], (D,), jnp.float32), 0.25, 1.75).astype(jnp.bfloat16),
        "w_query": draw_w_query(jax.random.fold_in(key_of[12], 71), 0),
        "w_key": noise(key_of[4], (D, KW), D ** -0.5, 0.25, ((0, 4),)),
        "w_value": noise(key_of[5], (D, KW), D ** -0.5, 0.25, ((0, 4),)),
        "w_out": noise(key_of[6], (QW, D), (max(QW // 64, 1)) ** -0.5, 2.0, ((1, 4),)),
        "mlp_gain": jnp.clip(1.0 + 0.15 * jax.random.normal(key_of[7], (D,), jnp.float32), 0.25, 1.75).astype(jnp.bfloat16),
        "w_gate": noise(key_of[8], (D, FF), D ** -0.5, 0.25, ((1, 4),)),
        "w_up": noise(key_of[9], (D, FF), D ** -0.5, 0.25, ((1, 4),)),
        "w_down": noise(key_of[10], (FF, D), FF ** -0.5, 0.15625, ((0, 4),)),
        "cotangent": noise(key_of[11], (TOKENS, D), 1.0, 6.0, ((0, 32),)),
    }


negative = -1e+30
epsilon = 1e-05
theta_base = 100000.0

def dot_last(left, right):
    return lax.dot_general(left, right, (((1,), (1,)), ((), ())), preferred_element_type=jnp.float32)

def dot_first(left, right):
    return lax.dot_general(left, right, (((0,), (0,)), ((), ())), preferred_element_type=jnp.float32)

def rms_forward(hidden, gain):
    scale = lax.rsqrt(lax.optimization_barrier(jnp.mean(hidden * hidden, axis=-1, keepdims=True)) + epsilon)
    return (hidden * scale * gain, scale)

def rms_backward(hidden, scale, gain, upstream):
    weighted = upstream * gain
    inner = lax.optimization_barrier(jnp.mean(weighted * hidden, axis=-1, keepdims=True))
    back = scale * weighted - hidden * (scale * scale * scale) * inner
    gain_grad = lax.optimization_barrier(jnp.sum(upstream * hidden * scale, axis=0))
    return (back, gain_grad)

def rope_tables(places, head_size):
    half = head_size // 2
    freqs = theta_base ** (-(jnp.arange(half, dtype=jnp.float32) * 2.0) / head_size)
    angle = places.astype(jnp.float32)[:, None] * freqs[None, :]
    cosine = jnp.cos(angle)
    sine = jnp.sin(angle)
    return (jnp.concatenate([cosine, cosine], -1), jnp.concatenate([sine, sine], -1))

def rotate(vectors, cosine, sine):
    half = vectors.shape[-1] // 2
    turned = jnp.concatenate([-vectors[..., half:], vectors[..., :half]], axis=-1)
    return vectors * cosine[:, None, :] + turned * sine[:, None, :]

def attend(query, key_rows, value_rows, allowed):
    factor = query.shape[-1] ** (-0.5)
    scores = jnp.einsum('qgd,sd->gqs', query.astype(jnp.float32), key_rows.astype(jnp.float32)) * factor
    scores = jnp.where(allowed[None], scores, negative)
    top = lax.optimization_barrier(jnp.max(scores, axis=-1, keepdims=True))
    log_total = top + jnp.log(lax.optimization_barrier(jnp.sum(jnp.exp(scores - top), axis=-1, keepdims=True)))
    probs = jnp.exp(scores - log_total).astype(jnp.bfloat16)
    mixed = jnp.einsum('gqs,sd->qgd', probs.astype(jnp.float32), value_rows.astype(jnp.float32))
    return (mixed.astype(jnp.bfloat16), log_total)

def attend_back(query, key_rows, value_rows, mixed, back_mixed, log_total, allowed):
    factor = query.shape[-1] ** (-0.5)
    scores = jnp.einsum('qgd,sd->gqs', query.astype(jnp.float32), key_rows.astype(jnp.float32)) * factor
    scores = jnp.where(allowed[None], scores, negative)
    probs = jnp.exp(scores - log_total)
    rounded = probs.astype(jnp.bfloat16).astype(jnp.float32)
    back_float = back_mixed.astype(jnp.float32)
    back_values = jnp.einsum('gqs,qgd->sd', rounded, back_float)
    back_probs = jnp.einsum('qgd,sd->gqs', back_float, value_rows.astype(jnp.float32))
    delta = lax.optimization_barrier(jnp.sum(back_float * mixed.astype(jnp.float32), axis=-1))
    back_scores = (probs * (back_probs - jnp.transpose(delta)[:, :, None]) * factor).astype(jnp.bfloat16)
    back_scores = back_scores.astype(jnp.float32)
    back_query = jnp.einsum('gqs,sd->qgd', back_scores, key_rows.astype(jnp.float32))
    back_keys = jnp.einsum('gqs,qgd->sd', back_scores, query.astype(jnp.float32))
    return (back_query, back_keys, back_values)

def reference(tokens, positions, attn_gain, w_query, w_key, w_value, w_out, mlp_gain, w_gate, w_up, w_down, cotangent):
    sharing = H // KVH
    gain_first = attn_gain.astype(jnp.float32)
    gain_second = mlp_gain.astype(jnp.float32)
    index = jnp.arange(SEQ, dtype=jnp.int32)

    def one_sequence(carry, item):
        seq_tokens, seq_places, seq_back = item
        wide = seq_tokens.astype(jnp.float32)
        normed_first, scale_first = rms_forward(wide, gain_first)
        normed_first = normed_first.astype(jnp.bfloat16)
        cosine, sine = rope_tables(seq_places, HD)
        query = rotate(jnp.dot(normed_first, w_query, preferred_element_type=jnp.float32).reshape(SEQ, H, HD), cosine, sine).astype(jnp.bfloat16)
        keys = rotate(jnp.dot(normed_first, w_key, preferred_element_type=jnp.float32).reshape(SEQ, KVH, HD), cosine, sine).astype(jnp.bfloat16)
        values = jnp.dot(normed_first, w_value, preferred_element_type=jnp.float32).astype(jnp.bfloat16)
        allowed = (index[None, :] <= index[:, None]) & (index[None, :] >= (index - seq_places)[:, None])
        query_groups = jnp.transpose(query.reshape(SEQ, KVH, sharing, HD), (1, 0, 2, 3))
        key_groups = jnp.transpose(keys, (1, 0, 2))
        value_groups = jnp.transpose(values.reshape(SEQ, KVH, HD), (1, 0, 2))

        def forward_group(parts):
            return attend(parts[0], parts[1], parts[2], allowed)
        mixed_groups, log_total = lax.map(forward_group, (query_groups, key_groups, value_groups))
        attended = jnp.transpose(mixed_groups, (1, 0, 2, 3)).reshape(SEQ, QW)
        hidden = wide + jnp.dot(attended, w_out, preferred_element_type=jnp.float32)
        normed_second, scale_second = rms_forward(hidden, gain_second)
        normed_second = normed_second.astype(jnp.bfloat16)
        gate = jnp.dot(normed_second, w_gate, preferred_element_type=jnp.float32)
        lifted = jnp.dot(normed_second, w_up, preferred_element_type=jnp.float32)
        sigmoid_gate = jax.nn.sigmoid(gate)
        activated = (gate * sigmoid_gate * lifted).astype(jnp.bfloat16)
        output = (hidden + jnp.dot(activated, w_down, preferred_element_type=jnp.float32)).astype(jnp.bfloat16)
        back_activated = dot_last(seq_back, w_down)
        grad_down = dot_first(activated, seq_back)
        back_gate = (back_activated * lifted * sigmoid_gate * (1.0 + gate * (1.0 - sigmoid_gate))).astype(jnp.bfloat16)
        back_lifted = (back_activated * gate * sigmoid_gate).astype(jnp.bfloat16)
        grad_gate = dot_first(normed_second, back_gate)
        grad_up = dot_first(normed_second, back_lifted)
        back_second = dot_last(back_gate, w_gate) + dot_last(back_lifted, w_up)
        back_mid, grad_mlp_gain = rms_backward(hidden, scale_second, gain_second, back_second)
        back_hidden = seq_back.astype(jnp.float32) + back_mid
        hidden_rounded = back_hidden.astype(jnp.bfloat16)
        grad_out = dot_first(attended, hidden_rounded)
        back_attended = dot_last(hidden_rounded, w_out).astype(jnp.bfloat16)
        back_groups = jnp.transpose(back_attended.reshape(SEQ, KVH, sharing, HD), (1, 0, 2, 3))

        def backward_group(parts):
            return attend_back(parts[0], parts[1], parts[2], parts[3], parts[4], parts[5], allowed)
        turned_q, turned_k, back_v = lax.map(backward_group, (query_groups, key_groups, value_groups, mixed_groups, back_groups, log_total))
        turned_query = jnp.transpose(turned_q, (1, 0, 2, 3)).reshape(SEQ, H, HD)
        turned_keys = jnp.transpose(turned_k, (1, 0, 2))
        back_values = jnp.transpose(back_v, (1, 0, 2)).reshape(SEQ, KW)
        back_query = rotate(turned_query, cosine, -sine).reshape(SEQ, QW).astype(jnp.bfloat16)
        back_keys = rotate(turned_keys, cosine, -sine).reshape(SEQ, KW).astype(jnp.bfloat16)
        back_values_low = back_values.astype(jnp.bfloat16)
        grad_query = dot_first(normed_first, back_query)
        grad_key = dot_first(normed_first, back_keys)
        grad_value = dot_first(normed_first, back_values_low)
        back_first = dot_last(back_query, w_query) + dot_last(back_keys, w_key) + dot_last(back_values_low, w_value)
        back_low, grad_attn_gain = rms_backward(wide, scale_first, gain_first, back_first)
        grad_tokens = back_hidden + back_low
        terms = (grad_attn_gain, grad_query, grad_key, grad_value, grad_out, grad_mlp_gain, grad_gate, grad_up, grad_down)
        carry = tuple((total + term for total, term in zip(carry, terms)))
        return (carry, (output, grad_tokens))
    shapes = (attn_gain, w_query, w_key, w_value, w_out, mlp_gain, w_gate, w_up, w_down)
    start = tuple((jnp.zeros(weight.shape, jnp.float32) for weight in shapes))
    items = (tokens.reshape(SEQS, SEQ, D), positions, cotangent.reshape(SEQS, SEQ, D))
    grads, (outputs, backs) = lax.scan(one_sequence, start, items)
    return (outputs.reshape(TOKENS, D), backs.reshape(TOKENS, D), grads[0], grads[1], grads[2], grads[3], grads[4], grads[5], grads[6], grads[7], grads[8])
```

```python
import jax
import jax.numpy as jnp
from jax import lax
from jax.sharding import PartitionSpec as P

H = 9
KVH = 3
HD = 64
QW = H * HD
KW = KVH * HD


negative = -1e30
epsilon = 1e-05
theta_base = 100000.0
f32 = jnp.float32
bf16 = jnp.bfloat16


def dot(left, right):
    return jnp.dot(left, right, preferred_element_type=f32)


def dot_last(left, right):
    return lax.dot_general(left, right, (((1,), (1,)), ((), ())), preferred_element_type=f32)


def dot_first(left, right):
    return lax.dot_general(left, right, (((0,), (0,)), ((), ())), preferred_element_type=f32)


def tie(value, *after):
    return lax.optimization_barrier((value,) + after)[0]


def rms_scale(hidden):
    return lax.rsqrt(jnp.mean(hidden * hidden, axis=-1, keepdims=True) + epsilon)


def rms_backward(hidden, scale, gain, upstream):
    weighted = upstream * gain
    inner = jnp.mean(weighted * hidden, axis=-1, keepdims=True)
    return scale * weighted - hidden * (scale * scale * scale) * inner


def rope_tables(places):
    half = HD // 2
    freqs = theta_base ** (-(jnp.arange(half, dtype=f32) * 2.0) / HD)
    angle = places[:, None] * freqs[None, :]
    cosine = jnp.cos(angle)
    sine = jnp.sin(angle)
    return (jnp.concatenate([cosine, cosine], -1), jnp.concatenate([sine, sine], -1))


def rotate(flat, cosine, sine):
    vectors = flat.reshape(flat.shape[0], -1, HD)
    half = HD // 2
    turned = jnp.concatenate([-vectors[..., half:], vectors[..., :half]], axis=-1)
    return (vectors * cosine[:, None, :] + turned * sine[:, None, :]).reshape(flat.shape)


def attend(query, key_rows, value_rows, allowed):
    factor = HD ** (-0.5)
    scores = jnp.einsum("qgd,sd->gqs", query, key_rows, preferred_element_type=f32) * factor
    scores = jnp.where(allowed[None], scores, negative)
    top = jnp.max(scores, axis=-1, keepdims=True)
    log_total = top + jnp.log(jnp.sum(jnp.exp(scores - top), axis=-1, keepdims=True))
    probs = jnp.exp(scores - log_total).astype(bf16)
    mixed = jnp.einsum("gqs,sd->qgd", probs, value_rows, preferred_element_type=f32)
    return (mixed.astype(bf16), log_total)


def attend_back(query, key_rows, value_rows, mixed, back_mixed, log_total, allowed):
    factor = HD ** (-0.5)
    scores = jnp.einsum("qgd,sd->gqs", query, key_rows, preferred_element_type=f32) * factor
    scores = jnp.where(allowed[None], scores, negative)
    probs = jnp.exp(scores - log_total)
    back_values = jnp.einsum("gqs,qgd->sd", probs.astype(bf16), back_mixed, preferred_element_type=f32)
    back_probs = jnp.einsum("qgd,sd->gqs", back_mixed, value_rows, preferred_element_type=f32)
    delta = jnp.sum(back_mixed.astype(f32) * mixed.astype(f32), axis=-1)
    back_scores = (probs * (back_probs - jnp.transpose(delta)[:, :, None]) * factor).astype(bf16)
    back_query = jnp.einsum("gqs,sd->qgd", back_scores, key_rows, preferred_element_type=f32)
    back_keys = jnp.einsum("gqs,qgd->sd", back_scores, query, preferred_element_type=f32)
    return (back_query, back_keys, back_values)


def factors_of(n):
    out = []
    if n > 4 or n == 2:
        out.append(2)
        n //= 2
    while n > 1:
        f = 4 if n % 4 == 0 else 2
        out.append(f)
        n //= f
    return out


def build(mesh):
    n_shard = mesh.shape["shard"]
    n_dp = mesh.shape["dp"]
    far = n_shard // 2

    def swap(axis, n, mask):
        pairs = [(i, i ^ mask) for i in range(n)]
        return lambda a: lax.ppermute(a, axis, pairs)

    core = swap("shard", n_shard, 1)
    cross = swap("shard", n_shard, far)

    def dp_sum(pieces):
        place = lax.axis_index("dp")
        stages = []
        stride = 1
        cur = pieces
        for f in factors_of(n_dp):
            digit = (place // stride) % f
            cur = cur.reshape((f, cur.shape[0] // f) + cur.shape[1:])
            low = cur.astype(bf16)
            got = [
                swap("dp", n_dp, k * stride)(lax.dynamic_index_in_dim(low, digit ^ k, 0, keepdims=False))
                for k in range(1, f)
            ]
            cur = lax.dynamic_index_in_dim(cur, digit, 0, keepdims=False).astype(f32)
            for g in got:
                cur = cur + g.astype(f32)
            stages.append((f, stride, digit))
            stride *= f
        cur = cur.astype(bf16)
        for f, stride, digit in reversed(stages):
            got = [cur] + [swap("dp", n_dp, k * stride)(cur) for k in range(1, f)]
            if f == 2:
                cur = jnp.where(digit == 0, jnp.stack(got), jnp.stack(got[::-1]))
            else:
                whole = jnp.zeros((f,) + cur.shape, cur.dtype)
                for k in range(f):
                    whole = lax.dynamic_update_index_in_dim(whole, got[k], digit ^ k, 0)
                cur = whole
            cur = cur.reshape((-1,) + cur.shape[2:])
        return cur

    def per_device(tokens, positions, attn_gain, w_query, w_key, w_value, w_out, mlp_gain, w_gate, w_up, w_down, cotangent):
        sharing = H // KVH
        count = tokens.shape[0]
        rows = attn_gain.shape[0]
        place = lax.axis_index("shard")

        def relative(a):
            mine = core(a)
            over = cross(a)
            return [a, mine, over, core(over)]

        def absolute(parts):
            lo = place % 2
            hi = place // 2
            a, b, c, d = parts
            near = jnp.where(lo == 0, jnp.stack([a, b]), jnp.stack([b, a]))
            away = jnp.where(lo == 0, jnp.stack([c, d]), jnp.stack([d, c]))
            return jnp.where(hi == 0, jnp.stack([near, away]), jnp.stack([away, near]))

        small = jnp.concatenate([positions[0].astype(f32), attn_gain.astype(f32), mlp_gain.astype(f32)])
        small_parts = relative(small)
        places4 = jnp.concatenate([p[:count] for p in small_parts])
        gains = absolute([p[count:].reshape(2, rows) for p in small_parts]).reshape(n_shard, 2, rows)
        gains = jnp.transpose(gains, (1, 0, 2)).reshape(2, n_shard * rows)
        gain_first, gain_second = gains[0], gains[1]

        qkv_own = jnp.concatenate([w_query, w_key, w_value], axis=1)
        qkv_parts = relative(qkv_own)
        token_parts = relative(tokens)
        full_qkv = absolute(qkv_parts).reshape(n_shard * rows, QW + 2 * KW)
        full_query = full_qkv[:, :QW]
        full_kv = full_qkv[:, QW:]
        out_t = tie(jnp.transpose(w_out), token_parts[2])
        full_out_t = absolute(relative(out_t)).reshape(n_shard * rows, QW)
        gate_other, up_other, down_other = [
            cross(tie(w, token_parts[2], qkv_parts[2])) for w in (w_gate, w_up, w_down)
        ]
        gate2 = jnp.concatenate([w_gate, gate_other], axis=1)
        up2 = jnp.concatenate([w_up, up_other], axis=1)
        down2 = jnp.concatenate([w_down, down_other], axis=0)
        cot2 = jnp.concatenate([cotangent, core(cotangent)], axis=0)

        tokens4 = jnp.concatenate(token_parts, axis=0)
        wide4 = tokens4.astype(f32)
        scale4 = rms_scale(wide4)
        normed4 = (wide4 * scale4 * gain_first).astype(bf16)
        wide = wide4[:count]
        scale_first = scale4[:count]
        cosine4, sine4 = rope_tables(places4)
        cosine, sine = cosine4[:count], sine4[:count]
        query = rotate(dot(normed4[:count], full_query), cosine, sine).astype(bf16)
        keyval = dot(normed4, full_kv)
        keys = rotate(keyval[:, :KW], cosine4, sine4).astype(bf16)
        values = keyval[:, KW:].astype(bf16)
        length = tokens4.shape[0]

        inside = jnp.arange(count, dtype=jnp.int32)
        query_index = place * count + inside
        key_index = jnp.concatenate([(place ^ r) * count + inside for r in range(n_shard)])
        first_index = query_index - positions[0]
        allowed = (key_index[None, :] <= query_index[:, None]) & (key_index[None, :] >= first_index[:, None])
        query_groups = query.reshape(count, KVH, sharing, HD)
        key_groups = keys.reshape(length, KVH, HD)
        value_groups = values.reshape(length, KVH, HD)

        mixed = []
        totals = []
        for g in range(KVH):
            m, t = attend(query_groups[:, g], key_groups[:, g], value_groups[:, g], allowed)
            mixed.append(m)
            totals.append(t)
        attended = jnp.stack(mixed, 1).reshape(count, QW)
        hidden = wide + dot_last(attended, full_out_t)
        scale_second = rms_scale(hidden)
        normed_second = (hidden * scale_second * gain_second).astype(bf16)
        ns2 = jnp.concatenate([normed_second, core(normed_second)], axis=0)
        gate = dot(ns2, gate2)
        lifted = dot(ns2, up2)
        sg = jax.nn.sigmoid(gate)
        activated = (gate * sg * lifted).astype(bf16)
        back_activated = dot_last(cot2, down2)
        back_gate = (back_activated * lifted * sg * (1.0 + gate * (1.0 - sg))).astype(bf16)
        back_lifted = (back_activated * gate * sg).astype(bf16)
        back_second2 = dot_last(back_gate, gate2) + dot_last(back_lifted, up2)
        back_second = back_second2[:count] + core(back_second2[count:].astype(bf16)).astype(f32)
        out2 = dot(activated, down2)
        output = (hidden + out2[:count] + core(out2[count:].astype(bf16)).astype(f32)).astype(bf16)
        own = w_gate.shape[1]
        grad_gate2 = dot_first(ns2, back_gate)
        grad_up2 = dot_first(ns2, back_lifted)
        grad_down2 = dot_first(activated, cot2)
        both = jnp.stack([grad_gate2[:, :own], grad_up2[:, :own]])
        both_other = jnp.stack([grad_gate2[:, own:], grad_up2[:, own:]]).astype(bf16)
        sum_both = both + cross(both_other).astype(f32)
        sum_both = dp_sum(sum_both.reshape(n_dp, -1, own)).reshape(both.shape).astype(f32)
        sum_down = grad_down2[:own] + cross(grad_down2[own:].astype(bf16)).astype(f32)
        sum_down = dp_sum(sum_down.reshape(n_dp, -1, sum_down.shape[1])).reshape(sum_down.shape).astype(f32)

        back_hidden = cotangent.astype(f32) + rms_backward(hidden, scale_second, gain_second, back_second)
        grad_mlp_gain = jnp.sum(back_second * hidden * scale_second, axis=0)
        hidden_rounded = back_hidden.astype(bf16)
        back_attended = dot(hidden_rounded, full_out_t).astype(bf16)

        def reduce_rows(partial):
            blocks = partial.reshape(n_shard, rows, -1)
            low = blocks.astype(bf16)

            def pick(stack, r):
                return lax.dynamic_index_in_dim(stack, place ^ r, 0, keepdims=False)

            got = core(jnp.stack([pick(low, 1), pick(low, far + 1)]))
            keep = pick(blocks, 0) + got[0].astype(f32)
            send = pick(blocks, far) + got[1].astype(f32)
            return keep + cross(send.astype(bf16)).astype(f32)

        def spread(flat):
            c = flat.shape[1]
            wide_c = -(-c // n_dp) * n_dp
            flat = jnp.pad(flat, ((0, 0), (0, wide_c - c)))
            return jnp.transpose(flat.reshape(flat.shape[0], n_dp, -1), (1, 0, 2))

        def unspread(pieces, c):
            flat = jnp.transpose(pieces, (1, 0, 2)).reshape(pieces.shape[1], -1)
            return flat[:, :c].astype(f32)

        grad_out_t = dot_first(hidden_rounded, attended)
        pack_out = jnp.concatenate([grad_out_t, grad_mlp_gain[:, None]], axis=1)
        sum_out = unspread(dp_sum(spread(reduce_rows(pack_out))), QW + 1)

        back_groups = back_attended.reshape(count, KVH, sharing, HD)
        turned_q, turned_k, back_v = [], [], []
        for g in range(KVH):
            a, b, c = attend_back(
                query_groups[:, g], key_groups[:, g], value_groups[:, g], mixed[g], back_groups[:, g], totals[g], allowed
            )
            turned_q.append(a)
            turned_k.append(b)
            back_v.append(c)
        turned_query = jnp.stack(turned_q, 1).reshape(count, QW)
        turned_keys = jnp.concatenate(turned_k, axis=1)
        back_values = jnp.concatenate(back_v, axis=1)
        back_query = rotate(turned_query, cosine, -sine).astype(bf16)
        back_kv4 = jnp.concatenate([rotate(turned_keys, cosine4, -sine4), back_values], axis=1)
        back_low4 = back_kv4.astype(bf16)
        grad_qkv = jnp.concatenate([dot_first(normed4[:count], back_query), dot_first(normed4, back_low4)], axis=1)
        sum_qkv = unspread(dp_sum(spread(reduce_rows(grad_qkv))), QW + 2 * KW)
        blocks = back_kv4.reshape(n_shard, count, 2 * KW)
        low = back_low4.reshape(n_shard, count, 2 * KW)
        got = core(jnp.stack([low[1], low[3]]))
        keep = blocks[0] + got[0].astype(f32)
        send = blocks[2] + got[1].astype(f32)
        back_kv = (keep + cross(send.astype(bf16)).astype(f32)).astype(bf16)
        back_first = dot_last(back_query, full_query) + dot_last(back_kv, full_kv)
        grad_tokens = back_hidden + rms_backward(wide, scale_first, gain_first, back_first)
        grad_attn_gain = jnp.sum(sum_qkv * qkv_own.astype(f32), axis=1) / attn_gain.astype(f32)
        return (
            output,
            grad_tokens,
            grad_attn_gain,
            sum_qkv[:, :QW],
            sum_qkv[:, QW : QW + KW],
            sum_qkv[:, QW + KW :],
            jnp.transpose(sum_out[:, :QW]),
            sum_out[:, QW],
            sum_both[0],
            sum_both[1],
            sum_down,
        )

    return per_device


def solution(mesh):
    rows = P(("dp", "shard"), None)
    first = P("shard", None)
    last = P(None, "shard")
    vec = P("shard")
    return jax.shard_map(
        build(mesh),
        mesh=mesh,
        in_specs=(rows, P("dp", "shard"), vec, first, first, first, last, vec, last, last, first, rows),
        out_specs=(rows, rows, vec, first, first, first, last, vec, last, last, first),
        check_vma=False,
    )
```
